256 devices in a mesh: rep: 4 (over z_hi), dom: 64 (over y, x, z_lo, core).
Axes of the slice: x: 4, y: 4, z: 8 (z_hi: 4, z_lo: 2; z = z_hi * 2 + z_lo), core: 2. Of those that a mesh axis runs over, the one named last changes fastest.
Arguments:
- cols: int32 [512, 8], P('dom', 'rep'), may hold values from 0 to 511, as said below
- vals: bfloat16 [512, 8, 128, 128], P('dom', 'rep')
- features: bfloat16 [65536, 128], P(('rep', 'dom')), may hold values from -6 to 6
- weight: bfloat16 [128, 128], replicated, may hold values from -0.5 to 0.5
- bias: float32 [128], replicated, may hold values from -3 to 3
- cotangent: bfloat16 [65536, 128], P('dom'), may hold values from -6 to 6
Outputs:
- output: bfloat16 [65536, 128], P('dom')
- feature_grad: float32 [65536, 128], P(('rep', 'dom'))
- weight_grad: float32 [128, 128], replicated
The draws below stay inside these ranges and needn't reach their ends.
Inputs may be any that keep to these rules, and one draw needn't show every extreme that they name: For every block row and every quarter q of the block columns, entries q * 2 to (q + 1) * 2 - 1 of its row of cols are 2 distinct block columns in the range q * 128 to (q + 1) * 128 - 1 (quarters as many as the size of rep); every block row names its own diagonal block.
All inputs are finite; a program needn't handle non-finite values.
Results may differ from the reference program's by a relative error of at most 0.0055.
Values may be sent and summed in bfloat16 or wider, within the bound.
A program may use at most 64 MiB of HBM per device.

```python
import jax
import jax.numpy as jnp
from jax import lax

F = 128
BS = 128
NBLK = 512
NODES = 65536
KQ = 2
N_REP = 4


def draw_cols(key, part):
    quarter_blocks = NBLK // N_REP
    scores = jax.random.randint(key, (NBLK, N_REP, quarter_blocks), 0, 1 << 20)
    slots = jnp.arange(quarter_blocks, dtype=jnp.int32)
    starts = (jnp.arange(N_REP, dtype=jnp.int32) * quarter_blocks)[None, :, None]
    targets = starts + slots[None, None, :]
    row_index = jnp.arange(NBLK, dtype=jnp.int32)[:, None, None]
    scores = scores * quarter_blocks + slots[None, None, :]
    scores = jnp.where(targets == row_index, -1, scores)
    order = jnp.argsort(scores, axis=2)[:, :, :KQ]
    return (order.astype(jnp.int32) + starts).reshape(NBLK, N_REP * KQ)


def draw_vals(key, part):
    shape = (NBLK, KQ * N_REP, BS, BS)
    key_values = jax.random.fold_in(key, 11)
    key_keep = jax.random.fold_in(key, 12)
    kept_of_sixteen = min(16, 128 // BS)
    entries = jnp.clip(jax.random.normal(key_values, shape, jnp.float32), -6.0, 6.0)
    keep = (jax.random.randint(key_keep, shape, 0, 16) < kept_of_sixteen).astype(jnp.float32)
    spread = (KQ * N_REP * BS * kept_of_sixteen / 16.0) ** (-0.5)
    return (entries * keep * spread).astype(jnp.bfloat16)


def block_scale(key, dims, shards, least, top_value):
    gain = 1.0
    for position, parts in shards:
        steps = jax.random.uniform(jax.random.fold_in(jax.random.fold_in(key, 6), position), (parts,), jnp.float32, least / len(shards), top_value / len(shards))
        gain = gain * jnp.repeat(jnp.exp(steps), dims[position] // parts).reshape((-1,) + (1,) * (len(dims) - 1 - position))
    return gain


def centred(own_key, dims, scale, reach, pieces=(), kind=jnp.bfloat16):
    values = jax.random.normal(own_key, dims, jnp.float32) * scale
    if len(pieces) > 0:
        values = block_scale(own_key, dims, pieces, -0.22, 0.18) * values
    return jnp.clip(values, min=-reach, max=reach).astype(kind)


def setup_inputs(seed: int = 0) -> dict:
    streams_of = jax.random.split(jax.random.key(seed), 7)
    cols = draw_cols(jax.random.fold_in(streams_of[6], 71), 0)
    vals = draw_vals(jax.random.fold_in(streams_of[6], 71), 0)
    features = centred(streams_of[2], (NODES, F), 1.0, 6.0, ((0, 256),))
    weight = centred(streams_of[3], (F, F), F ** -0.5, 0.5)
    bias = centred(streams_of[4], (F,), 0.5, 3.0, (), jnp.float32)
    cotangent = centred(streams_of[5], (NODES, F), 1.0, 6.0, ((0, 64),))
    return {"cols": cols, "vals": vals, "features": features, "weight": weight, "bias": bias, "cotangent": cotangent}


def reference(cols, vals, features, weight, bias, cotangent):
    blocks = features.reshape(NBLK, BS, F)

    def row_sum(item):
        row_cols, row_vals = item
        picked = blocks[row_cols].astype(jnp.float32)
        return jnp.einsum('kij,kjf->if', row_vals.astype(jnp.float32), picked)

    summed = lax.map(row_sum, (cols, vals)).reshape(NODES, F)
    aggregated = summed.astype(jnp.bfloat16)
    hidden = jnp.dot(aggregated, weight, preferred_element_type=jnp.float32) + bias
    gate_prob = jax.nn.sigmoid(hidden)
    output = (hidden * gate_prob).astype(jnp.bfloat16)
    grad_hidden = (cotangent.astype(jnp.float32) * gate_prob * (1.0 + hidden * (1.0 - gate_prob))).astype(jnp.bfloat16)
    weight_grad = jnp.dot(aggregated.T, grad_hidden, preferred_element_type=jnp.float32)
    grad_agg = jnp.dot(grad_hidden, weight.T, preferred_element_type=jnp.float32).astype(jnp.bfloat16)
    grad_rows = grad_agg.reshape(NBLK, BS, F)

    def scatter_row(total, item):
        row_cols, row_vals, row_grad = item
        terms = jnp.einsum('kij,if->kjf', row_vals.astype(jnp.float32), row_grad.astype(jnp.float32))
        return total.at[row_cols].add(terms), None

    start_total = jnp.zeros((NBLK, BS, F), jnp.float32)
    feature_grad, _ = lax.scan(scatter_row, start_total, (cols, vals, grad_rows))
    return output, feature_grad.reshape(NODES, F), weight_grad
```

```python
import jax
import jax.numpy as jnp
from jax import lax
from jax.experimental import pallas as pl
from jax.experimental.pallas import tpu as pltpu
from jax.sharding import PartitionSpec as P

MESH = pl.DeviceIdType.MESH
F32 = jnp.float32
BF16 = jnp.bfloat16
BS = 128
ORDER = (2, 1, 3, 0)
SENDS = 200


def kernel(
    cols_ref, vals_ref, feat_ref, weight_ref, bias_ref, cot_ref,
    out_ref, fgrad_ref, wgrad_ref,
    cols_s, first_s, next_s,
    vals_v, vals_t, weight_v, bias_v, cot_v, first_v,
    quart, part, part_in, agg, grad, out_v,
    wpart, wsib, wa, wb, wz, wr, wfull,
    acc, acc_b, acc_sib,
    dense, relay_in, final_in, summed, relay2_in, final2_in, tail, tail_b, tail_in, fg_v,
    load_sem, send_sem, ag_sem, agsib_sem, tab_sem, rep_sem, repag_sem, w_sem, accsib_sem,
    relay_sem, final_sem, relay2_sem, final2_sem, tail_sem,
):
    rep = lax.axis_index("rep")
    dom = lax.axis_index("dom")
    y, x, z, c = dom // 16, (dom // 4) % 4, (dom // 2) % 2, dom % 2
    pa = x + c * (y - x)
    pb = y + c * (x - y)

    def flat(qa, qb, qz):
        qx = qa + c * (qb - qa)
        qy = qb + c * (qa - qb)
        return (qy * 4 + qx) * 2 + qz

    def off(da, db):
        return (pa + da) % 4, (pb + db) % 4

    def device(da=0, db=0, qz=None, core=None, drep=0):
        qa, qb = off(da, db)
        i = flat(qa, qb, z if qz is None else qz)
        return ((rep + drep) % 4, i * 2 + (c if core is None else core))

    sib = device(core=1 - c)
    zpeer = device(qz=1 - z)
    started = []

    def send(src, dst, sem, target):
        n = len(started)
        copy = pltpu.make_async_remote_copy(
            src_ref=src, dst_ref=dst, send_sem=send_sem.at[n], recv_sem=sem, device_id=target, device_id_type=MESH
        )
        copy.start()
        started.append(copy)

    def arrive(dst, sem):
        pltpu.make_async_remote_copy(
            src_ref=dst, dst_ref=dst, send_sem=send_sem.at[0], recv_sem=sem, device_id=sib, device_id_type=MESH
        ).wait_recv()

    loads = []

    def load(src, dst):
        copy = pltpu.make_async_copy(src, dst, load_sem.at[len(loads)])
        copy.start()
        loads.append(copy)
        return copy

    own = flat(pa, pb, z)
    own_slot = quart.at[pl.ds((own * 2 + c) * 2, 2)]
    load_cols = load(cols_ref, cols_s)
    load_feat = load(feat_ref, own_slot)
    load_vals = load(vals_ref, vals_v)
    load_weight = load(weight_ref, weight_v)
    load_bias = load(bias_ref, bias_v)
    load_cot = load(cot_ref, cot_v)

    barrier = pltpu.get_barrier_semaphore()
    partners = [sib, zpeer]
    partners += [device(da=k) for k in (1, 2, 3)]
    partners += [device(db=k) for k in (1, 2, 3)]
    partners += [device(drep=k) for k in (1, 2, 3)]
    for partner in partners:
        pl.semaphore_signal(barrier, inc=1, device_id=partner, device_id_type=MESH)
    pl.semaphore_wait(barrier, len(partners))

    def shard(i):
        return quart.at[pl.ds((i * 2 + c) * 2, 2)]

    def half(i, h):
        return quart.at[pl.ds((i * 2 + c) * 2 + h, 1)]

    def to_axis(i, da, db, src=None):
        send(shard(i) if src is None else src, shard(i), ag_sem.at[i, 0], device(da=da, db=db))

    def to_sib(i, src=None):
        send(shard(i) if src is None else src, shard(i), agsib_sem.at[i], sib)

    def got(i):
        arrive(shard(i), ag_sem.at[i, 0])

    def got_half(i, h):
        arrive(half(i, h), ag_sem.at[i, h])

    for da, db in ((0, 1), (0, 3), (1, 0), (3, 0)):
        to_axis(own, da, db, feat_ref)
    send(feat_ref, shard(own), ag_sem.at[own, 0], zpeer)
    to_sib(own, feat_ref)

    load_cols.wait()
    column = [lax.rem(cols_s[t % 2, t // 2], 128) for t in range(16)]
    lane = lax.broadcasted_iota(jnp.int32, (1, 128), 1)
    first = jnp.full((1, 128), 16, jnp.int32)
    for t in reversed(range(16)):
        first = jnp.where(lane == column[t], t, first)
    first_v[0] = first
    send(first_v.at[0], first_v.at[1], tab_sem, sib)

    def a_shard(da, qz):
        i = flat((pa + da) % 4, pb, qz)
        if da == 2:
            got_half(i, 0)
            got_half(i, 1)
        else:
            got(i)
            h, onward = (0, 1) if da == 3 else (1, 3)
            send(half(i, h), half(i, h), ag_sem.at[i, h], device(da=onward))
        to_axis(i, 0, 1)
        to_axis(i, 0, 3)
        to_sib(i)

    def b_shard(da, db, qz):
        qa, qb = off(da, db)
        i = flat(qa, qb, qz)
        if db == 2:
            got_half(i, 0)
            got_half(i, 1)
        else:
            got(i)
            h, onward = (0, 1) if db == 3 else (1, 3)
            send(half(i, h), half(i, h), ag_sem.at[i, h], device(db=onward))
        to_sib(i)

    across = flat(pa, pb, 1 - z)
    got(across)
    for da, db in ((0, 1), (0, 3), (1, 0), (3, 0)):
        to_axis(across, da, db)
    to_sib(across)
    a_shard(3, z)
    a_shard(1, z)
    b_shard(0, 3, z)
    b_shard(0, 1, z)
    a_shard(3, 1 - z)
    a_shard(1, 1 - z)
    b_shard(0, 3, 1 - z)
    b_shard(0, 1, 1 - z)
    a_shard(2, z)
    a_shard(2, 1 - z)

    load_vals.wait()

    def transpose(t):
        vals_t[t] = vals_v[t].T

    todo = list(range(16))
    for da, qz in ((3, z), (1, z), (3, 1 - z), (1, 1 - z), (2, z), (2, 1 - z)):
        for db in (3, 1):
            b_shard(da, db, qz)
            if todo:
                transpose(todo.pop(0))
    for t in range(16):
        following = jnp.int32(16)
        for u in reversed(range(t + 1, 16)):
            if u // 2 != t // 2:
                following = jnp.where(column[u] == column[t], u, following)
        next_s[t] = following
    for da in (0, 3, 1, 2):
        for qz in (z, 1 - z):
            b_shard(da, 2, qz)
            if todo:
                transpose(todo.pop(0))
    acc[16] = jnp.zeros((BS, BS), F32)
    acc_b[16] = jnp.zeros((BS, BS), BF16)
    acc_sib[16] = jnp.zeros((BS, BS), BF16)
    arrive(first_v.at[1], tab_sem)
    table_copy = pltpu.make_async_copy(first_v, first_s, load_sem.at[6])
    table_copy.start()
    load_feat.wait()
    for i in range(32):
        arrive(quart.at[pl.ds((i * 2 + 1 - c) * 2, 2)], agsib_sem.at[i])

    def row_sum(row):
        left = jnp.dot(vals_v[row * 2], quart[lax.rem(cols_s[0, row], 128)], preferred_element_type=F32)
        right = jnp.dot(vals_v[row * 2 + 1], quart[lax.rem(cols_s[1, row], 128)], preferred_element_type=F32)
        return left + right

    own_sum = []
    for k in ORDER:
        s = (rep + k) % 4
        for j in range(2):
            total = row_sum(s * 2 + j)
            if k == 0:
                own_sum.append(total)
            else:
                part[k, j] = total.astype(BF16)
        if k:
            send(part.at[k], part_in.at[k], rep_sem.at[k], device(drep=k))
    for k in (1, 3, 2):
        arrive(part_in.at[k], rep_sem.at[k])
    for j in range(2):
        total = own_sum[j] + (
            part_in[1, j].astype(F32) + part_in[3, j].astype(F32) + part_in[2, j].astype(F32)
        )
        agg[rep, pl.ds(j * BS, BS)] = total.astype(BF16)
    for k in (2, 1, 3):
        send(agg.at[rep], agg.at[rep], repag_sem.at[k], device(drep=k))

    load_weight.wait()
    load_bias.wait()
    load_cot.wait()
    stores = []

    def store(src, dst):
        copy = pltpu.make_async_copy(src, dst, load_sem.at[7 + len(stores)])
        copy.start()
        stores.append(copy)

    def layer(s):
        rows = agg[s]
        hidden = jnp.dot(rows, weight_v[...], preferred_element_type=F32) + bias_v[...]
        gate = jax.nn.sigmoid(hidden)
        out_v[s] = (hidden * gate).astype(BF16)
        grad_hidden = (cot_v[s].astype(F32) * gate * (1.0 + hidden * (1.0 - gate))).astype(BF16)
        grad_rows = lax.dot_general(
            grad_hidden, weight_v[...], (((1,), (1,)), ((), ())), preferred_element_type=F32
        )
        grad[s] = grad_rows.astype(BF16)
        store(out_v.at[s], out_ref.at[s])
        return rows, grad_hidden

    rows, grad_hidden = layer(rep)
    product = lax.dot_general(rows, grad_hidden, (((0,), (0,)), ((), ())), preferred_element_type=F32)
    wpart[0] = product[:64]
    wpart[1] = product[64:]
    send(wpart.at[1 - c], wsib, w_sem.at[0], sib)
    for k in (3, 1, 2):
        arrive(agg.at[(rep + 4 - k) % 4], repag_sem.at[k])
        layer((rep + 4 - k) % 4)

    def w_stage_a():
        arrive(wsib, w_sem.at[0])
        wa[pa] = wpart[c] + wsib[...]
        for k in (1, 2, 3):
            send(wa.at[pa], wa.at[pa], w_sem.at[k], device(da=k))

    def w_stage_b():
        for k in (1, 2, 3):
            arrive(wa.at[(pa + 4 - k) % 4], w_sem.at[k])
        wb[pb] = (wa[0] + wa[1]) + (wa[2] + wa[3])
        for k in (1, 2, 3):
            send(wb.at[pb], wb.at[pb], w_sem.at[3 + k], device(db=k))

    def w_stage_z():
        for k in (1, 2, 3):
            arrive(wb.at[(pb + 4 - k) % 4], w_sem.at[3 + k])
        wz[z] = (wb[0] + wb[1]) + (wb[2] + wb[3])
        send(wz.at[z], wz.at[z], w_sem.at[7], zpeer)

    def w_stage_rep():
        arrive(wz.at[1 - z], w_sem.at[7])
        wr[rep] = wz[0] + wz[1]
        for k in (1, 2, 3):
            send(wr.at[rep], wr.at[rep], w_sem.at[7 + k], device(drep=k))

    def w_stage_sib():
        for k in (1, 2, 3):
            arrive(wr.at[(rep + 4 - k) % 4], w_sem.at[7 + k])
        wfull[c] = (wr[0] + wr[1]) + (wr[2] + wr[3])
        send(wfull.at[c], wfull.at[c], w_sem.at[11], sib)

    def w_done():
        arrive(wfull.at[1 - c], w_sem.at[11])
        store(wfull, wgrad_ref)

    w_stage_a()

    for t in reversed(range(16)):
        row = t // 2
        term = jnp.dot(vals_t[t], grad[row // 2, pl.ds((row % 2) * BS, BS)], preferred_element_type=F32)
        term = term + acc[next_s[t]]
        acc[t] = term
        acc_b[t] = term.astype(BF16)
        if t % 4 == 0:
            send(acc_b.at[pl.ds(t, 4)], acc_sib.at[pl.ds(t, 4)], accsib_sem.at[t // 4], sib)
    table_copy.wait()
    w_stage_b()
    for q in range(4):
        arrive(acc_sib.at[pl.ds(q * 4, 4)], accsib_sem.at[q])

    def place(ob, oa, blk=0, zz=0):
        return ((ob * 4 + oa) * 2 + blk) * 2 + zz

    def build(ob, oa):
        qa, qb = off(oa, ob)
        for blk in range(2):
            for zz in range(2):
                j = (flat(qa, qb, zz) * 2 + c) * 2 + blk
                dense[place(ob, oa, blk, zz)] = acc_b[first_s[0, 0, j]] + acc_sib[first_s[1, 0, j]]

    def pair(ob, oa, blk):
        return dense.at[pl.ds(place(ob, oa, blk), 2)]

    for oa in ORDER:
        build(2, oa)
        send(pair(2, oa, 0), relay_in.at[0, oa], relay_sem.at[0, oa], device(db=1))
        send(pair(2, oa, 1), relay_in.at[1, oa], relay_sem.at[1, oa], device(db=3))
    for oa in ORDER:
        build(1, oa)
        send(pair(1, oa, 1), final_in.at[0, oa, 1], final_sem.at[0, oa, 1], device(db=1))
        build(3, oa)
        send(pair(3, oa, 0), final_in.at[1, oa, 0], final_sem.at[1, oa, 0], device(db=3))
    for oa in ORDER:
        for side, ob, blk in ((0, 1, 0), (1, 3, 1)):
            arrive(relay_in.at[side, oa], relay_sem.at[side, oa])
            at = pl.ds(place(ob, oa, blk), 2)
            dense[at] = (dense[at].astype(F32) + relay_in[side, oa].astype(F32)).astype(BF16)
            send(pair(ob, oa, blk), final_in.at[side, oa, blk], final_sem.at[side, oa, blk], device(db=ob))
    w_stage_z()
    for oa in ORDER:
        build(0, oa)

    def sum_b(oa):
        for side in range(2):
            for blk in range(2):
                arrive(final_in.at[side, oa, blk], final_sem.at[side, oa, blk])
        for blk in range(2):
            total = dense[pl.ds(place(0, oa, blk), 2)].astype(F32) + (
                final_in[0, oa, blk].astype(F32) + final_in[1, oa, blk].astype(F32)
            )
            summed[oa, blk] = total.astype(BF16)

    sum_b(2)
    send(summed.at[2, 0], relay2_in.at[0], relay2_sem.at[0], device(da=1))
    send(summed.at[2, 1], relay2_in.at[1], relay2_sem.at[1], device(da=3))
    w_stage_rep()
    sum_b(1)
    send(summed.at[1, 1], final2_in.at[0, 1], final2_sem.at[0, 1], device(da=1))
    sum_b(3)
    send(summed.at[3, 0], final2_in.at[1, 0], final2_sem.at[1, 0], device(da=3))
    for side, oa, blk in ((0, 1, 0), (1, 3, 1)):
        arrive(relay2_in.at[side], relay2_sem.at[side])
        summed[oa, blk] = (summed[oa, blk].astype(F32) + relay2_in[side].astype(F32)).astype(BF16)
        send(summed.at[oa, blk], final2_in.at[side, blk], final2_sem.at[side, blk], device(da=oa))
    sum_b(0)
    w_stage_sib()
    for side in range(2):
        for blk in range(2):
            arrive(final2_in.at[side, blk], final2_sem.at[side, blk])
    for blk in range(2):
        for zz in range(2):
            total = summed[0, blk, zz].astype(F32) + (
                final2_in[0, blk, zz].astype(F32) + final2_in[1, blk, zz].astype(F32)
            )
            tail[zz, blk] = total
            tail_b[zz, blk] = total.astype(BF16)
    send(tail_b.at[1 - z], tail_in, tail_sem, zpeer)
    w_done()
    arrive(tail_in, tail_sem)
    fg_v[...] = tail[z] + tail_in[...].astype(F32)
    store(fg_v, fgrad_ref)
    for copy in started:
        copy.wait_send()
    for copy in stores:
        copy.wait()


def body(cols, vals, features, weight, bias, cotangent):
    anywhere = pl.BlockSpec(memory_space=pl.ANY)
    vmem = pltpu.VMEM
    dma = pltpu.SemaphoreType.DMA
    block = (BS, BS)
    scratch = [
        pltpu.SMEM((2, 8), jnp.int32),
        pltpu.SMEM((2, 1, 128), jnp.int32),
        pltpu.SMEM((16,), jnp.int32),
        vmem((16, *block), BF16),
        vmem((16, *block), BF16),
        vmem(block, BF16),
        vmem((1, BS), F32),
        vmem((4, 256, BS), BF16),
        vmem((2, 1, 128), jnp.int32),
        vmem((128, *block), BF16),
        vmem((4, 2, *block), BF16),
        vmem((4, 2, *block), BF16),
        vmem((4, 256, BS), BF16),
        vmem((4, 256, BS), BF16),
        vmem((4, 256, BS), BF16),
        vmem((2, 64, BS), F32),
        vmem((64, BS), F32),
        vmem((4, 64, BS), F32),
        vmem((4, 64, BS), F32),
        vmem((2, 64, BS), F32),
        vmem((4, 64, BS), F32),
        vmem((2, 64, BS), F32),
        vmem((17, *block), F32),
        vmem((17, *block), BF16),
        vmem((17, *block), BF16),
        vmem((64, *block), BF16),
        vmem((2, 4, 2, *block), BF16),
        vmem((2, 4, 2, 2, *block), BF16),
        vmem((4, 2, 2, *block), BF16),
        vmem((2, 2, *block), BF16),
        vmem((2, 2, 2, *block), BF16),
        vmem((2, 2, *block), F32),
        vmem((2, 2, *block), BF16),
        vmem((2, *block), BF16),
        vmem((2, *block), F32),
        dma((16,)),
        dma((SENDS,)),
        dma((32, 2)),
        dma((32,)),
        dma,
        dma((4,)),
        dma((4,)),
        dma((12,)),
        dma((4,)),
        dma((2, 4)),
        dma((2, 4, 2)),
        dma((2,)),
        dma((2, 2)),
        dma,
    ]
    output, feature_grad, weight_grad = pl.pallas_call(
        kernel,
        out_shape=(
            jax.ShapeDtypeStruct((4, 256, BS), BF16),
            jax.ShapeDtypeStruct((2, *block), F32),
            jax.ShapeDtypeStruct((2, 64, BS), F32),
        ),
        in_specs=[anywhere] * 6,
        out_specs=(anywhere,) * 3,
        scratch_shapes=scratch,
        compiler_params=pltpu.CompilerParams(
            collective_id=0, has_side_effects=True, vmem_limit_bytes=32 << 20
        ),
    )(
        cols.T,
        vals.reshape(16, *block),
        features.reshape(2, *block),
        weight,
        bias.reshape(1, BS),
        cotangent.reshape(4, 256, BS),
    )
    return output.reshape(1024, BS), feature_grad.reshape(256, BS), weight_grad.reshape(BS, BS)


def solution(mesh):
    placed = (
        P("dom", "rep"),
        P("dom", "rep", None, None),
        P(("rep", "dom"), None),
        P(),
        P(),
        P("dom", None),
    )
    return jax.shard_map(
        body,
        mesh=mesh,
        in_specs=placed,
        out_specs=(P("dom", None), P(("rep", "dom"), None), P()),
        check_vma=False,
    )
```

```python
import jax
import jax.numpy as jnp
from jax import lax
from jax.experimental import pallas as pl
from jax.experimental.pallas import tpu as pltpu
from jax.sharding import PartitionSpec as P

MESH = pl.DeviceIdType.MESH
F32 = jnp.float32
BF16 = jnp.bfloat16
BS = 128
ORDER = (2, 1, 3, 0)
DIRECT = ((2, 1),)


def kernel(
    cols_ref, vals_ref, feat_ref, weight_ref, bias_ref, cot_ref,
    out_ref, fgrad_ref, wgrad_ref,
    cols_s, first_s, next_s,
    vals_v, vals_t, weight_v, bias_v, cot_v, first_v,
    quart, part, part_in, agg, out_v,
    wpart, wsib, wa, wb, wr, wfull,
    acc, acc_b, acc_sib,
    dense, relay_in, final_in, summed, near_in, fg_v,
    load_sem, send_sem, ag_sem, agsib_sem, tab_sem, rep_sem, repag_sem, w_sem, accsib_sem,
    relay_sem, final_sem, near_sem,
):
    rep = lax.axis_index("rep")
    dom = lax.axis_index("dom")
    y, x, z, c = dom // 16, (dom // 4) % 4, (dom // 2) % 2, dom % 2
    pa = x + c * (y - x)
    pb = y + c * (x - y)

    def flat(qa, qb, qz):
        qx = qa + c * (qb - qa)
        qy = qb + c * (qa - qb)
        return (qy * 4 + qx) * 2 + qz

    def spot(da, db, dz):
        return flat((pa + da) % 4, (pb + db) % 4, (z + dz) % 2)

    def device(da=0, db=0, dz=0, core=None, drep=0):
        return ((rep + drep) % 4, spot(da, db, dz) * 2 + (c if core is None else core))

    sib = device(core=1 - c)
    sent = [0, 0, 0]

    def send(src, dst, sem, target, group=2, blocks=1):
        pltpu.make_async_remote_copy(
            src_ref=src, dst_ref=dst, send_sem=send_sem.at[group], recv_sem=sem, device_id=target, device_id_type=MESH
        ).start()
        sent[group] += blocks

    def arrive(dst, sem):
        pltpu.make_async_remote_copy(
            src_ref=dst, dst_ref=dst, send_sem=send_sem.at[0], recv_sem=sem, device_id=sib, device_id_type=MESH
        ).wait_recv()

    loads = []

    def load(src, dst):
        copy = pltpu.make_async_copy(src, dst, load_sem.at[len(loads)])
        copy.start()
        loads.append(copy)
        return copy

    own = spot(0, 0, 0)
    load_feat = load(feat_ref, quart.at[pl.ds((own * 2 + c) * 2, 2)])
    load_cols = load(cols_ref, cols_s)
    load_vals = load(vals_ref, vals_v)
    load_weight = load(weight_ref, weight_v)
    load_bias = load(bias_ref, bias_v)
    load_cot = load(cot_ref, cot_v)

    near = [(1, 0), (3, 0), (0, 1), (2, 0), (1, 1), (3, 1), (2, 1)]
    barrier = pltpu.get_barrier_semaphore()
    partners = [sib]
    partners += [device(da=da, dz=dz) for da, dz in near]
    partners += [device(db=k) for k in (1, 2, 3)]
    partners += [device(drep=k) for k in (1, 2, 3)]
    for partner in partners:
        pl.semaphore_signal(barrier, inc=1, device_id=partner, device_id_type=MESH)
    load_feat.wait()
    pl.semaphore_wait(barrier, len(partners))

    def shard(i):
        return quart.at[pl.ds((i * 2 + c) * 2, 2)]

    def half(i, h):
        return quart.at[pl.ds((i * 2 + c) * 2 + h, 1)]

    def half_sem(i, h):
        return ag_sem.at[h * 32 + i]

    def to_axis(i, **where):
        send(shard(i), shard(i), ag_sem.at[i], device(**where), 1, 2)

    def to_sib(i):
        send(shard(i), shard(i), agsib_sem, sib, 0, 2)

    def along_b(da, dz):
        i = spot(da, 0, dz)
        to_axis(i, db=1)
        to_axis(i, db=3)
        if (da, dz) in DIRECT:
            to_axis(i, db=2)
        to_sib(i)

    along_b(0, 0)
    for da, dz in near:
        to_axis(own, da=da, dz=dz)

    arrivals = [(k, j) for j in range(2) for k in (1, 3, 2)]
    order = ([(0, 0), (0, 1)] + arrivals)[::-1]
    rows = [((rep + 4 - k) % 4) * 2 + j for k, j in order]
    load_cols.wait()
    column = [lax.rem(cols_s[t % 2, rows[t // 2]], 128) for t in range(16)]
    lane = lax.broadcasted_iota(jnp.int32, (1, 128), 1)
    first = jnp.full((1, 128), 16, jnp.int32)
    for t in reversed(range(16)):
        first = jnp.where(lane == column[t], t, first)
    first_v[0] = first
    first_copy = pltpu.make_async_remote_copy(
        src_ref=first_v.at[0], dst_ref=first_v.at[1], send_sem=send_sem.at[3], recv_sem=tab_sem,
        device_id=sib, device_id_type=MESH,
    )
    first_copy.start()

    def near_shard(da, dz):
        i = spot(da, 0, dz)
        arrive(shard(i), ag_sem.at[i])
        along_b(da, dz)

    def beside(da, dz):
        for db, h, onward in ((3, 0, 1), (1, 1, 3)):
            i = spot(da, db, dz)
            arrive(shard(i), ag_sem.at[i])
            if (da, dz) not in DIRECT:
                send(half(i, h), half(i, h), half_sem(i, h), device(db=onward), 1, 1)
            to_sib(i)

    def opposite(da, dz):
        i = spot(da, 2, dz)
        if (da, dz) in DIRECT:
            arrive(shard(i), ag_sem.at[i])
        else:
            arrive(half(i, 0), half_sem(i, 0))
            arrive(half(i, 1), half_sem(i, 1))
        to_sib(i)

    load_vals.wait()
    todo = list(range(16))

    def transpose(n):
        for _ in range(n):
            t = todo.pop(0)
            vals_t[t] = vals_v[rows[t // 2] * 2 + t % 2].T

    transpose(4)
    near_shard(1, 0)
    near_shard(3, 0)
    near_shard(0, 1)
    beside(0, 0)
    near_shard(2, 0)
    near_shard(1, 1)
    near_shard(3, 1)
    beside(1, 0)
    beside(3, 0)
    beside(0, 1)
    near_shard(2, 1)
    transpose(2)
    beside(2, 0)
    transpose(2)
    beside(1, 1)
    transpose(2)
    beside(3, 1)
    transpose(2)
    opposite(0, 0)
    transpose(2)
    opposite(1, 0)
    transpose(2)
    opposite(3, 0)
    for t in range(16):
        following = jnp.int32(16)
        for u in reversed(range(t + 1, 16)):
            if u // 2 != t // 2:
                following = jnp.where(column[u] == column[t], u, following)
        next_s[t] = following
    acc[16] = jnp.zeros((BS, BS), F32)
    acc_b[16] = jnp.zeros((BS, BS), BF16)
    acc_sib[16] = jnp.zeros((BS, BS), BF16)
    arrive(first_v.at[1], tab_sem)
    table_copy = pltpu.make_async_copy(first_v, first_s, load_sem.at[6])
    table_copy.start()
    opposite(0, 1)
    opposite(2, 0)
    beside(2, 1)
    opposite(1, 1)
    opposite(3, 1)
    opposite(2, 1)
    arrive(quart.at[pl.ds(0, 64)], agsib_sem)

    def row_sum(row):
        left = jnp.dot(vals_v[row * 2], quart[lax.rem(cols_s[0, row], 128)], preferred_element_type=F32)
        right = jnp.dot(vals_v[row * 2 + 1], quart[lax.rem(cols_s[1, row], 128)], preferred_element_type=F32)
        return left + right

    own_sum = []
    for j in range(2):
        for k in ORDER:
            total = row_sum(((rep + k) % 4) * 2 + j)
            if k == 0:
                own_sum.append(total)
            else:
                part[k, j] = total.astype(BF16)
                send(part.at[k, j], part_in.at[k, j], rep_sem.at[k, j], device(drep=k))

    def reduce_rep(j):
        for k in (1, 3, 2):
            arrive(part_in.at[k, j], rep_sem.at[k, j])
        total = own_sum[j] + (
            part_in[1, j].astype(F32) + part_in[3, j].astype(F32) + part_in[2, j].astype(F32)
        )
        agg[rep * 2 + j] = total.astype(BF16)
        for k in (2, 1, 3):
            send(agg.at[rep * 2 + j], agg.at[rep * 2 + j], repag_sem.at[k, j], device(drep=k))

    def layer(pos):
        row = rows[pos]
        mine = agg[row]
        hidden = jnp.dot(mine, weight_v[...], preferred_element_type=F32) + bias_v[...]
        gate = jax.nn.sigmoid(hidden)
        out_v[row] = (hidden * gate).astype(BF16)
        pltpu.make_async_copy(out_v.at[row], out_ref.at[row], load_sem.at[7]).start()
        grad_hidden = (cot_v[row].astype(F32) * gate * (1.0 + hidden * (1.0 - gate))).astype(BF16)
        grad_rows = lax.dot_general(
            grad_hidden, weight_v[...], (((1,), (1,)), ((), ())), preferred_element_type=F32
        ).astype(BF16)
        for t in (pos * 2 + 1, pos * 2):
            term = jnp.dot(vals_t[t], grad_rows, preferred_element_type=F32) + acc[next_s[t]]
            acc[t] = term
            acc_b[t] = term.astype(BF16)
        send(acc_b.at[pl.ds(pos * 2, 2)], acc_sib.at[pl.ds(pos * 2, 2)], accsib_sem, sib, 2, 2)
        return lax.dot_general(mine, grad_hidden, (((0,), (0,)), ((), ())), preferred_element_type=F32) if pos > 5 else None

    def w_stage_near():
        arrive(wsib, w_sem.at[0])
        wa[pa * 2 + z] = wpart[c] + wsib[...]
        for n, (da, dz) in enumerate(near):
            send(wa.at[pa * 2 + z], wa.at[pa * 2 + z], w_sem.at[1 + n], device(da=da, dz=dz))

    def w_stage_b():
        for n, (da, dz) in enumerate(near):
            arrive(wa.at[((pa + 4 - da) % 4) * 2 + (z + dz) % 2], w_sem.at[1 + n])
        wb[pb] = ((wa[0] + wa[1]) + (wa[2] + wa[3])) + ((wa[4] + wa[5]) + (wa[6] + wa[7]))
        for k in (1, 2, 3):
            send(wb.at[pb], wb.at[pb], w_sem.at[7 + k], device(db=k))

    def w_stage_rep():
        for k in (1, 2, 3):
            arrive(wb.at[(pb + 4 - k) % 4], w_sem.at[7 + k])
        wr[rep] = (wb[0] + wb[1]) + (wb[2] + wb[3])
        for k in (1, 2, 3):
            send(wr.at[rep], wr.at[rep], w_sem.at[10 + k], device(drep=k))

    def w_stage_sib():
        for k in (1, 2, 3):
            arrive(wr.at[(rep + 4 - k) % 4], w_sem.at[10 + k])
        wfull[c] = (wr[0] + wr[1]) + (wr[2] + wr[3])
        send(wfull.at[c], wfull.at[c], w_sem.at[14], sib)

    load_weight.wait()
    load_bias.wait()
    load_cot.wait()
    reduce_rep(0)
    product = layer(7)
    reduce_rep(1)
    product = product + layer(6)
    wpart[0] = product[:64]
    wpart[1] = product[64:]
    send(wpart.at[1 - c], wsib, w_sem.at[0], sib)
    for n, (k, j) in enumerate(arrivals):
        arrive(agg.at[rows[5 - n]], repag_sem.at[k, j])
        layer(5 - n)
        if n == 1:
            w_stage_near()
    table_copy.wait()
    arrive(acc_sib.at[pl.ds(0, 16)], accsib_sem)

    def place(ob, oa, zz):
        return ((ob * 4 + oa) * 2 + zz) * 2

    def build(ob, oa):
        for zz in range(2):
            i = flat((pa + oa) % 4, (pb + ob) % 4, zz)
            for blk in range(2):
                j = (i * 2 + c) * 2 + blk
                dense[place(ob, oa, zz) + blk] = acc_b[first_s[0, 0, j]] + acc_sib[first_s[1, 0, j]]

    def to_b(oa, ob, zz):
        side = 0 if ob == 1 else 1
        send(
            dense.at[pl.ds(place(ob, oa, zz), 2)], final_in.at[side, oa, zz], final_sem.at[side, oa], device(db=ob), 2, 2
        )

    for oa in ORDER:
        build(2, oa)
        send(dense.at[pl.ds(place(2, oa, 0), 2)], relay_in.at[0, oa], relay_sem.at[0, oa], device(db=1), 2, 2)
        send(dense.at[pl.ds(place(2, oa, 1), 2)], relay_in.at[1, oa], relay_sem.at[1, oa], device(db=3), 2, 2)
    for n, oa in enumerate(ORDER):
        build(1, oa)
        build(3, oa)
        if n == 0:
            to_b(oa, 1, 1)
            to_b(oa, 3, 0)
    w_stage_b()
    for n, oa in enumerate(ORDER):
        for side, ob, zz in ((0, 1, 0), (1, 3, 1)):
            arrive(relay_in.at[side, oa], relay_sem.at[side, oa])
            at = pl.ds(place(ob, oa, zz), 2)
            dense[at] = (dense[at].astype(F32) + relay_in[side, oa].astype(F32)).astype(BF16)
            to_b(oa, ob, zz)
        if n < 3:
            to_b(ORDER[n + 1], 1, 1)
            to_b(ORDER[n + 1], 3, 0)
    for oa in ORDER:
        build(0, oa)

    for oa in ORDER:
        for side in range(2):
            arrive(final_in.at[side, oa], final_sem.at[side, oa])
        for zz in range(2):
            total = dense[pl.ds(place(0, oa, zz), 2)].astype(F32) + (
                final_in[0, oa, zz].astype(F32) + final_in[1, oa, zz].astype(F32)
            )
            summed[oa, zz] = total.astype(BF16)
            if oa == 0:
                fg_v[zz] = total
        for dz in (1, 0):
            if oa or dz:
                slot = oa * 2 + dz
                send(summed.at[oa, (z + dz) % 2], near_in.at[slot], near_sem.at[slot], device(da=oa, dz=dz), 2, 2)
        if oa == 2:
            w_stage_rep()
    w_stage_sib()
    total = fg_v[z]
    for oa in ORDER:
        for dz in (0, 1):
            if oa or dz:
                slot = oa * 2 + dz
                arrive(near_in.at[slot], near_sem.at[slot])
                total = total + near_in[slot].astype(F32)
    fg_v[2] = total
    fgrad_copy = pltpu.make_async_copy(fg_v.at[2], fgrad_ref, load_sem.at[8])
    fgrad_copy.start()
    arrive(wfull.at[1 - c], w_sem.at[14])
    wgrad_copy = pltpu.make_async_copy(wfull, wgrad_ref, load_sem.at[9])
    wgrad_copy.start()
    for group, blocks in enumerate(sent):
        assert blocks <= 128
        ref = quart.at[pl.ds(0, blocks)]
        pltpu.make_async_remote_copy(
            src_ref=ref, dst_ref=ref, send_sem=send_sem.at[group], recv_sem=tab_sem, device_id=sib, device_id_type=MESH
        ).wait_send()
    first_copy.wait_send()
    pltpu.make_async_copy(out_v, out_ref, load_sem.at[7]).wait()
    fgrad_copy.wait()
    wgrad_copy.wait()


def emit(out_in, fgrad_in, wgrad_in, out_ref, fgrad_ref, wgrad_ref, sem):
    copies = [
        pltpu.make_async_copy(src, dst, sem.at[n])
        for n, (src, dst) in enumerate(((out_in, out_ref), (fgrad_in, fgrad_ref), (wgrad_in, wgrad_ref)))
    ]
    for copy in copies:
        copy.start()
    for copy in copies:
        copy.wait()


def body(cols, vals, features, weight, bias, cotangent):
    anywhere = pl.BlockSpec(memory_space=pl.ANY)
    vmem = pltpu.VMEM
    dma = pltpu.SemaphoreType.DMA
    block = (BS, BS)
    scratch = [
        pltpu.SMEM((2, 8), jnp.int32),
        pltpu.SMEM((2, 1, 128), jnp.int32),
        pltpu.SMEM((16,), jnp.int32),
        vmem((16, *block), BF16),
        vmem((16, *block), BF16),
        vmem(block, BF16),
        vmem((1, BS), F32),
        vmem((8, *block), BF16),
        vmem((2, 1, 128), jnp.int32),
        vmem((128, *block), BF16),
        vmem((4, 2, *block), BF16),
        vmem((4, 2, *block), BF16),
        vmem((8, *block), BF16),
        vmem((8, *block), BF16),
        vmem((2, 64, BS), F32),
        vmem((64, BS), F32),
        vmem((8, 64, BS), F32),
        vmem((4, 64, BS), F32),
        vmem((4, 64, BS), F32),
        vmem((2, 64, BS), F32),
        vmem((17, *block), F32),
        vmem((17, *block), BF16),
        vmem((17, *block), BF16),
        vmem((64, *block), BF16),
        vmem((2, 4, 2, *block), BF16),
        vmem((2, 4, 2, 2, *block), BF16),
        vmem((4, 2, 2, *block), BF16),
        vmem((8, 2, *block), BF16),
        vmem((3, 2, *block), F32),
        dma((10,)),
        dma((4,)),
        dma((64,)),
        dma,
        dma,
        dma((4, 2)),
        dma((4, 2)),
        dma((15,)),
        dma,
        dma((2, 4)),
        dma((2, 4)),
        dma((8,)),
    ]
    results = (
        jax.ShapeDtypeStruct((8, *block), BF16),
        jax.ShapeDtypeStruct((2, *block), F32),
        jax.ShapeDtypeStruct((2, 64, BS), F32),
    )
    operands = (
        cols.T,
        vals.reshape(16, *block),
        features.reshape(2, *block),
        weight,
        bias.reshape(1, BS),
        cotangent.reshape(8, *block),
    )
    outs = pl.pallas_call(
        kernel,
        out_shape=results,
        in_specs=[anywhere] * 6,
        out_specs=(anywhere,) * 3,
        scratch_shapes=scratch,
        compiler_params=pltpu.CompilerParams(
            collective_id=0, has_side_effects=True, vmem_limit_bytes=32 << 20
        ),
    )(*[pltpu.with_memory_space_constraint(operand, pltpu.HBM) for operand in operands])
    output, feature_grad, weight_grad = pl.pallas_call(
        emit,
        out_shape=results,
        in_specs=[anywhere] * 3,
        out_specs=(anywhere,) * 3,
        scratch_shapes=[dma((3,))],
    )(*[pltpu.with_memory_space_constraint(out, pltpu.VMEM) for out in outs])
    return output.reshape(1024, BS), feature_grad.reshape(256, BS), weight_grad.reshape(BS, BS)


def solution(mesh):
    placed = (
        P("dom", "rep"),
        P("dom", "rep", None, None),
        P(("rep", "dom"), None),
        P(),
        P(),
        P("dom", None),
    )
    return jax.shard_map(
        body,
        mesh=mesh,
        in_specs=placed,
        out_specs=(P("dom", None), P(("rep", "dom"), None), P()),
        check_vma=False,
    )
```

```python
import jax
import jax.numpy as jnp
from jax import lax
from jax.experimental import pallas as pl
from jax.experimental.pallas import tpu as pltpu
from jax.sharding import PartitionSpec as P

MESH = pl.DeviceIdType.MESH
F32 = jnp.float32
BF16 = jnp.bfloat16
BS = 128
ORDER = (2, 1, 3, 0)
DIRECT = ((2, 1),)


def kernel(
    cols_ref, vals_ref, feat_ref, weight_ref, bias_ref, cot_ref,
    out_ref, fgrad_ref, wgrad_ref,
    cols_s, first_s, next_s,
    vals_v, vals_sib, vals_t, weight_v, bias_v, cot_v, first_v,
    quart, cross, cross_in, part, part_in, agg, out_v,
    wpart, wsib, wa, wb, wr, wfull,
    acc, acc_b, acc_sib,
    dense, relay_in, final_in, summed, near_in, fg_v,
    load_sem, send_sem, ag_sem, cross_sem, vals_sem, tab_sem, rep_sem, repag_sem, w_sem, accsib_sem,
    relay_sem, final_sem, near_sem,
):
    rep = lax.axis_index("rep")
    dom = lax.axis_index("dom")
    y, x, z, c = dom // 16, (dom // 4) % 4, (dom // 2) % 2, dom % 2
    pa = x + c * (y - x)
    pb = y + c * (x - y)

    def flat(qa, qb, qz):
        qx = qa + c * (qb - qa)
        qy = qb + c * (qa - qb)
        return (qy * 4 + qx) * 2 + qz

    def spot(da, db, dz):
        return flat((pa + da) % 4, (pb + db) % 4, (z + dz) % 2)

    def device(da=0, db=0, dz=0, core=None, drep=0):
        return ((rep + drep) % 4, spot(da, db, dz) * 2 + (c if core is None else core))

    sib = device(core=1 - c)
    sent = [0, 0, 0]

    def send(src, dst, sem, target, group=2, blocks=1):
        pltpu.make_async_remote_copy(
            src_ref=src, dst_ref=dst, send_sem=send_sem.at[group], recv_sem=sem, device_id=target, device_id_type=MESH
        ).start()
        sent[group] += blocks

    def arrive(dst, sem):
        pltpu.make_async_remote_copy(
            src_ref=dst, dst_ref=dst, send_sem=send_sem.at[0], recv_sem=sem, device_id=sib, device_id_type=MESH
        ).wait_recv()

    loads = []

    def load(src, dst):
        copy = pltpu.make_async_copy(src, dst, load_sem.at[len(loads)])
        copy.start()
        loads.append(copy)
        return copy

    own = spot(0, 0, 0)
    load_feat = load(feat_ref, quart.at[pl.ds((own * 2 + c) * 2, 2)])
    load_cols = load(cols_ref, cols_s)
    load_vals = load(vals_ref, vals_v)
    load_weight = load(weight_ref, weight_v)
    load_bias = load(bias_ref, bias_v)
    load_cot = load(cot_ref, cot_v)

    near = [(1, 0), (3, 0), (0, 1), (2, 0), (1, 1), (3, 1), (2, 1)]
    barrier = pltpu.get_barrier_semaphore()
    partners = [sib]
    partners += [device(da=da, dz=dz) for da, dz in near]
    partners += [device(db=k) for k in (1, 2, 3)]
    partners += [device(drep=k) for k in (1, 2, 3)]
    for partner in partners:
        pl.semaphore_signal(barrier, inc=1, device_id=partner, device_id_type=MESH)
    load_feat.wait()
    pl.semaphore_wait(barrier, len(partners))

    def shard(i):
        return quart.at[pl.ds((i * 2 + c) * 2, 2)]

    def half(i, h):
        return quart.at[pl.ds((i * 2 + c) * 2 + h, 1)]

    def half_sem(i, h):
        return ag_sem.at[h * 32 + i]

    def to_axis(i, **where):
        send(shard(i), shard(i), ag_sem.at[i], device(**where), 1, 2)

    def along_b(da, dz):
        i = spot(da, 0, dz)
        to_axis(i, db=1)
        to_axis(i, db=3)
        if (da, dz) in DIRECT:
            to_axis(i, db=2)

    along_b(0, 0)
    for da, dz in near:
        to_axis(own, da=da, dz=dz)

    arrivals = [(k, j) for j in range(2) for k in (1, 3, 2)]
    order = ([(0, 0), (0, 1)] + arrivals)[::-1]
    rows = [((rep + 4 - k) % 4) * 2 + j for k, j in order]
    load_cols.wait()
    column = [lax.rem(cols_s[t % 2, rows[t // 2]], 128) for t in range(16)]
    lane = lax.broadcasted_iota(jnp.int32, (1, 128), 1)
    first = jnp.full((1, 128), 16, jnp.int32)
    for t in reversed(range(16)):
        first = jnp.where(lane == column[t], t, first)
    spots = jnp.zeros((1, 128), jnp.int32)
    for row in range(8):
        for k in range(2):
            spots = jnp.where(lane == row * 2 + k, lax.rem(cols_s[k, row], 128), spots)
    first_v[0, 0] = first
    first_v[0, 1] = spots
    first_copy = pltpu.make_async_remote_copy(
        src_ref=first_v.at[0], dst_ref=first_v.at[1], send_sem=send_sem.at[3], recv_sem=tab_sem,
        device_id=sib, device_id_type=MESH,
    )
    first_copy.start()

    def near_shard(da, dz):
        i = spot(da, 0, dz)
        arrive(shard(i), ag_sem.at[i])
        along_b(da, dz)

    def beside(da, dz):
        for db, h, onward in ((3, 0, 1), (1, 1, 3)):
            i = spot(da, db, dz)
            arrive(shard(i), ag_sem.at[i])
            if (da, dz) not in DIRECT:
                send(half(i, h), half(i, h), half_sem(i, h), device(db=onward), 1, 1)

    def opposite(da, dz):
        i = spot(da, 2, dz)
        if (da, dz) in DIRECT:
            arrive(shard(i), ag_sem.at[i])
        else:
            arrive(half(i, 0), half_sem(i, 0))
            arrive(half(i, 1), half_sem(i, 1))

    load_vals.wait()
    send(vals_v, vals_sib, vals_sem, sib, 0, 16)
    todo = list(range(16))

    def transpose(n):
        for _ in range(n):
            t = todo.pop(0)
            vals_t[t] = vals_v[rows[t // 2] * 2 + t % 2].T

    transpose(4)
    near_shard(1, 0)
    near_shard(3, 0)
    near_shard(0, 1)
    beside(0, 0)
    near_shard(2, 0)
    near_shard(1, 1)
    near_shard(3, 1)
    beside(1, 0)
    beside(3, 0)
    beside(0, 1)
    near_shard(2, 1)
    transpose(2)
    beside(2, 0)
    transpose(2)
    beside(1, 1)
    transpose(2)
    beside(3, 1)
    transpose(2)
    opposite(0, 0)
    transpose(2)
    opposite(1, 0)
    transpose(2)
    opposite(3, 0)
    for t in range(16):
        following = jnp.int32(16)
        for u in reversed(range(t + 1, 16)):
            if u // 2 != t // 2:
                following = jnp.where(column[u] == column[t], u, following)
        next_s[t] = following
    acc[16] = jnp.zeros((BS, BS), F32)
    acc_b[16] = jnp.zeros((BS, BS), BF16)
    acc_sib[16] = jnp.zeros((BS, BS), BF16)
    quart[128] = jnp.zeros((BS, BS), BF16)
    arrive(first_v.at[1], tab_sem)
    table_copy = pltpu.make_async_copy(first_v, first_s, load_sem.at[6])
    table_copy.start()
    opposite(0, 1)
    opposite(2, 0)
    beside(2, 1)
    opposite(1, 1)
    opposite(3, 1)
    opposite(2, 1)
    arrive(vals_sib, vals_sem)
    table_copy.wait()

    def row_sum(vals, side, row):
        held = []
        for k in range(2):
            spot_at = first_s[side, 1, 0, row * 2 + k]
            held.append(quart[jnp.where((spot_at // 2) % 2 == c, spot_at, 128)])
        wide = jnp.concatenate([vals[row * 2], vals[row * 2 + 1]], axis=1)
        return jnp.dot(wide, jnp.concatenate(held, axis=0), preferred_element_type=F32)

    def targets(j):
        return [(k, ((rep + k) % 4) * 2 + j) for k in ORDER]

    for j in range(2):
        for k, row in targets(j):
            cross[k, j] = row_sum(vals_sib, 1, row)
        for k in ORDER:
            send(cross.at[k, j], cross_in.at[k, j], cross_sem.at[k, j], sib, 0, 2)
    own_sum = []
    for j in range(2):
        totals = [row_sum(vals_v, 0, row) for _, row in targets(j)]
        for k in ORDER:
            arrive(cross_in.at[k, j], cross_sem.at[k, j])
        for k, total in zip(ORDER, totals):
            total = total + cross_in[k, j]
            if k == 0:
                own_sum.append(total)
            else:
                part[k, j] = total.astype(BF16).reshape(2, 64, BS)
        for q in range(2):
            for k in (2, 1, 3):
                send(part.at[k, j, q], part_in.at[k, j, q], rep_sem.at[k - 1, j * 2 + q], device(drep=k), 0, 0.5)

    def reduce_rep(j, q):
        for k in (1, 3, 2):
            arrive(part_in.at[k, j, q], rep_sem.at[k - 1, j * 2 + q])
        total = own_sum[j][q * 64 : q * 64 + 64] + (
            part_in[1, j, q].astype(F32) + part_in[3, j, q].astype(F32) + part_in[2, j, q].astype(F32)
        )
        agg[rep * 2 + j, q] = total.astype(BF16)
        for k in (2, 1, 3):
            piece = agg.at[rep * 2 + j, q]
            send(piece, piece, repag_sem.at[k - 1, j * 2 + q], device(drep=k), 0, 0.5)

    def layer(pos):
        row = rows[pos]
        mine = agg[row].reshape(BS, BS)
        hidden = jnp.dot(mine, weight_v[...], preferred_element_type=F32) + bias_v[...]
        gate = jax.nn.sigmoid(hidden)
        out_v[row] = (hidden * gate).astype(BF16)
        pltpu.make_async_copy(out_v.at[row], out_ref.at[row], load_sem.at[7]).start()
        grad_hidden = (cot_v[row].astype(F32) * gate * (1.0 + hidden * (1.0 - gate))).astype(BF16)
        grad_rows = lax.dot_general(
            grad_hidden, weight_v[...], (((1,), (1,)), ((), ())), preferred_element_type=F32
        ).astype(BF16)
        for t in (pos * 2 + 1, pos * 2):
            term = jnp.dot(vals_t[t], grad_rows, preferred_element_type=F32) + acc[next_s[t]]
            acc[t] = term
            acc_b[t] = term.astype(BF16)
        send(acc_b.at[pl.ds(pos * 2, 2)], acc_sib.at[pl.ds(pos * 2, 2)], accsib_sem, sib, 2, 2)
        return lax.dot_general(mine, grad_hidden, (((0,), (0,)), ((), ())), preferred_element_type=F32) if pos > 5 else None

    def w_stage_near():
        arrive(wsib, w_sem.at[0])
        wa[pa * 2 + z] = wpart[c] + wsib[...]
        for n, (da, dz) in enumerate(near):
            send(wa.at[pa * 2 + z], wa.at[pa * 2 + z], w_sem.at[1 + n], device(da=da, dz=dz))

    def w_stage_b():
        for n, (da, dz) in enumerate(near):
            arrive(wa.at[((pa + 4 - da) % 4) * 2 + (z + dz) % 2], w_sem.at[1 + n])
        wb[pb] = ((wa[0] + wa[1]) + (wa[2] + wa[3])) + ((wa[4] + wa[5]) + (wa[6] + wa[7]))
        for k in (1, 2, 3):
            send(wb.at[pb], wb.at[pb], w_sem.at[7 + k], device(db=k))

    def w_stage_rep():
        for k in (1, 2, 3):
            arrive(wb.at[(pb + 4 - k) % 4], w_sem.at[7 + k])
        wr[rep] = (wb[0] + wb[1]) + (wb[2] + wb[3])
        for k in (1, 2, 3):
            send(wr.at[rep], wr.at[rep], w_sem.at[10 + k], device(drep=k))

    def w_stage_sib():
        for k in (1, 2, 3):
            arrive(wr.at[(rep + 4 - k) % 4], w_sem.at[10 + k])
        wfull[c] = (wr[0] + wr[1]) + (wr[2] + wr[3])
        send(wfull.at[c], wfull.at[c], w_sem.at[14], sib)

    load_weight.wait()
    load_bias.wait()
    load_cot.wait()
    reduce_rep(0, 0)
    reduce_rep(0, 1)
    product = layer(7)
    reduce_rep(1, 0)
    reduce_rep(1, 1)
    product = product + layer(6)
    wpart[0] = product[:64]
    wpart[1] = product[64:]
    send(wpart.at[1 - c], wsib, w_sem.at[0], sib)
    for n, (k, j) in enumerate(arrivals):
        for q in range(2):
            arrive(agg.at[rows[5 - n], q], repag_sem.at[k - 1, j * 2 + q])
        layer(5 - n)
        if n == 1:
            w_stage_near()
    arrive(acc_sib.at[pl.ds(0, 16)], accsib_sem)

    def place(ob, oa, zz):
        return ((ob * 4 + oa) * 2 + zz) * 2

    def build(ob, oa):
        for zz in range(2):
            i = flat((pa + oa) % 4, (pb + ob) % 4, zz)
            for blk in range(2):
                j = (i * 2 + c) * 2 + blk
                dense[place(ob, oa, zz) + blk] = acc_b[first_s[0, 0, 0, j]] + acc_sib[first_s[1, 0, 0, j]]

    def to_b(oa, ob, zz):
        side = 0 if ob == 1 else 1
        send(
            dense.at[pl.ds(place(ob, oa, zz), 2)], final_in.at[side, oa, zz], final_sem.at[side, oa], device(db=ob), 2, 2
        )

    for oa in ORDER:
        build(2, oa)
        send(dense.at[pl.ds(place(2, oa, 0), 2)], relay_in.at[0, oa], relay_sem.at[0, oa], device(db=1), 2, 2)
        send(dense.at[pl.ds(place(2, oa, 1), 2)], relay_in.at[1, oa], relay_sem.at[1, oa], device(db=3), 2, 2)
    for n, oa in enumerate(ORDER):
        build(1, oa)
        build(3, oa)
        if n == 0:
            to_b(oa, 1, 1)
            to_b(oa, 3, 0)
    w_stage_b()
    for n, oa in enumerate(ORDER):
        for side, ob, zz in ((0, 1, 0), (1, 3, 1)):
            arrive(relay_in.at[side, oa], relay_sem.at[side, oa])
            at = pl.ds(place(ob, oa, zz), 2)
            dense[at] = (dense[at].astype(F32) + relay_in[side, oa].astype(F32)).astype(BF16)
            to_b(oa, ob, zz)
        if n < 3:
            to_b(ORDER[n + 1], 1, 1)
            to_b(ORDER[n + 1], 3, 0)
    w_stage_rep()
    for oa in ORDER:
        build(0, oa)

    for oa in ORDER:
        for side in range(2):
            arrive(final_in.at[side, oa], final_sem.at[side, oa])
        for zz in range(2):
            total = dense[pl.ds(place(0, oa, zz), 2)].astype(F32) + (
                final_in[0, oa, zz].astype(F32) + final_in[1, oa, zz].astype(F32)
            )
            summed[oa, zz] = total.astype(BF16)
            if oa == 0:
                fg_v[zz] = total
        for dz in (1, 0):
            if oa or dz:
                slot = oa * 2 + dz
                send(summed.at[oa, (z + dz) % 2], near_in.at[slot], near_sem.at[slot], device(da=oa, dz=dz), 2, 2)
    w_stage_sib()
    total = fg_v[z]
    for oa in ORDER:
        for dz in (0, 1):
            if oa or dz:
                slot = oa * 2 + dz
                arrive(near_in.at[slot], near_sem.at[slot])
                total = total + near_in[slot].astype(F32)
    fg_v[2] = total
    fgrad_copy = pltpu.make_async_copy(fg_v.at[2], fgrad_ref, load_sem.at[8])
    fgrad_copy.start()
    arrive(wfull.at[1 - c], w_sem.at[14])
    wgrad_copy = pltpu.make_async_copy(wfull, wgrad_ref, load_sem.at[9])
    wgrad_copy.start()
    for group, blocks in enumerate(sent):
        assert blocks <= 128 and blocks == int(blocks)
        ref = quart.at[pl.ds(0, int(blocks))]
        pltpu.make_async_remote_copy(
            src_ref=ref, dst_ref=ref, send_sem=send_sem.at[group], recv_sem=tab_sem, device_id=sib, device_id_type=MESH
        ).wait_send()
    first_copy.wait_send()
    pltpu.make_async_copy(out_v, out_ref, load_sem.at[7]).wait()
    fgrad_copy.wait()
    wgrad_copy.wait()


def emit(out_in, fgrad_in, wgrad_in, out_ref, fgrad_ref, wgrad_ref, sem):
    copies = [
        pltpu.make_async_copy(src, dst, sem.at[n])
        for n, (src, dst) in enumerate(((out_in, out_ref), (fgrad_in, fgrad_ref), (wgrad_in, wgrad_ref)))
    ]
    for copy in copies:
        copy.start()
    for copy in copies:
        copy.wait()


def body(cols, vals, features, weight, bias, cotangent):
    anywhere = pl.BlockSpec(memory_space=pl.ANY)
    vmem = pltpu.VMEM
    dma = pltpu.SemaphoreType.DMA
    block = (BS, BS)
    scratch = [
        pltpu.SMEM((2, 8), jnp.int32),
        pltpu.SMEM((2, 2, 1, 128), jnp.int32),
        pltpu.SMEM((16,), jnp.int32),
        vmem((16, *block), BF16),
        vmem((16, *block), BF16),
        vmem((16, *block), BF16),
        vmem(block, BF16),
        vmem((1, BS), F32),
        vmem((8, *block), BF16),
        vmem((2, 2, 1, 128), jnp.int32),
        vmem((129, *block), BF16),
        vmem((4, 2, *block), F32),
        vmem((4, 2, *block), F32),
        vmem((4, 2, 2, 64, BS), BF16),
        vmem((4, 2, 2, 64, BS), BF16),
        vmem((8, 2, 64, BS), BF16),
        vmem((8, *block), BF16),
        vmem((2, 64, BS), F32),
        vmem((64, BS), F32),
        vmem((8, 64, BS), F32),
        vmem((4, 64, BS), F32),
        vmem((4, 64, BS), F32),
        vmem((2, 64, BS), F32),
        vmem((17, *block), F32),
        vmem((17, *block), BF16),
        vmem((17, *block), BF16),
        vmem((64, *block), BF16),
        vmem((2, 4, 2, *block), BF16),
        vmem((2, 4, 2, 2, *block), BF16),
        vmem((4, 2, 2, *block), BF16),
        vmem((8, 2, *block), BF16),
        vmem((3, 2, *block), F32),
        dma((10,)),
        dma((4,)),
        dma((64,)),
        dma((4, 2)),
        dma,
        dma,
        dma((3, 4)),
        dma((3, 4)),
        dma((15,)),
        dma,
        dma((2, 4)),
        dma((2, 4)),
        dma((8,)),
    ]
    results = (
        jax.ShapeDtypeStruct((8, *block), BF16),
        jax.ShapeDtypeStruct((2, *block), F32),
        jax.ShapeDtypeStruct((2, 64, BS), F32),
    )
    operands = (
        cols.T,
        vals.reshape(16, *block),
        features.reshape(2, *block),
        weight,
        bias.reshape(1, BS),
        cotangent.reshape(8, *block),
    )
    outs = pl.pallas_call(
        kernel,
        out_shape=results,
        in_specs=[anywhere] * 6,
        out_specs=(anywhere,) * 3,
        scratch_shapes=scratch,
        compiler_params=pltpu.CompilerParams(
            collective_id=0, has_side_effects=True, vmem_limit_bytes=32 << 20
        ),
    )(*[pltpu.with_memory_space_constraint(operand, pltpu.HBM) for operand in operands])
    output, feature_grad, weight_grad = pl.pallas_call(
        emit,
        out_shape=results,
        in_specs=[anywhere] * 3,
        out_specs=(anywhere,) * 3,
        scratch_shapes=[dma((3,))],
    )(*[pltpu.with_memory_space_constraint(out, pltpu.VMEM) for out in outs])
    return output.reshape(1024, BS), feature_grad.reshape(256, BS), weight_grad.reshape(BS, BS)


def solution(mesh):
    placed = (
        P("dom", "rep"),
        P("dom", "rep", None, None),
        P(("rep", "dom"), None),
        P(),
        P(),
        P("dom", None),
    )
    return jax.shard_map(
        body,
        mesh=mesh,
        in_specs=placed,
        out_specs=(P("dom", None), P(("rep", "dom"), None), P()),
        check_vma=False,
    )
```

```python
import jax
import jax.numpy as jnp
from jax import lax
from jax.experimental import pallas as pl
from jax.experimental.pallas import tpu as pltpu
from jax.sharding import PartitionSpec as P

MESH = pl.DeviceIdType.MESH
F32 = jnp.float32
BF16 = jnp.bfloat16
BS = 128
ORDER = (2, 1, 3, 0)
DIRECT = ((2, 1),)


def kernel(
    cols_ref, vals_ref, feat_ref, weight_ref, bias_ref, cot_ref,
    out_ref, fgrad_ref, wgrad_ref,
    cols_s, first_s, next_s,
    vals_v, vals_sib, vals_t, weight_v, bias_v, cot_v, first_v,
    quart, cross, cross_in, part, part_in, agg, out_v,
    wpart, wsib, wa, wb, wr, wfull,
    acc, acc_b, acc_sib,
    dense, relay_in, final_in, summed, near_in, fg_v,
    load_sem, send_sem, ag_sem, cross_sem, vals_sem, tab_sem, rep_sem, repag_sem, w_sem, accsib_sem,
    relay_sem, final_sem, last_sem, near_sem,
):
    rep = lax.axis_index("rep")
    dom = lax.axis_index("dom")
    y, x, z, c = dom // 16, (dom // 4) % 4, (dom // 2) % 2, dom % 2
    pa = x + c * (y - x)
    pb = y + c * (x - y)

    def flat(qa, qb, qz):
        qx = qa + c * (qb - qa)
        qy = qb + c * (qa - qb)
        return (qy * 4 + qx) * 2 + qz

    def spot(da, db, dz):
        return flat((pa + da) % 4, (pb + db) % 4, (z + dz) % 2)

    def device(da=0, db=0, dz=0, core=None, drep=0):
        return ((rep + drep) % 4, spot(da, db, dz) * 2 + (c if core is None else core))

    sib = device(core=1 - c)
    sent = [0, 0, 0]

    def send(src, dst, sem, target, group=2, blocks=1):
        pltpu.make_async_remote_copy(
            src_ref=src, dst_ref=dst, send_sem=send_sem.at[group], recv_sem=sem, device_id=target, device_id_type=MESH
        ).start()
        sent[group] += blocks

    def arrive(dst, sem):
        pltpu.make_async_remote_copy(
            src_ref=dst, dst_ref=dst, send_sem=send_sem.at[0], recv_sem=sem, device_id=sib, device_id_type=MESH
        ).wait_recv()

    loads = []

    def load(src, dst):
        copy = pltpu.make_async_copy(src, dst, load_sem.at[len(loads)])
        copy.start()
        loads.append(copy)
        return copy

    own = spot(0, 0, 0)
    load_feat = load(feat_ref, quart.at[pl.ds((own * 2 + c) * 2, 2)])
    load_cols = load(cols_ref, cols_s)
    load_vals = load(vals_ref, vals_v)
    load_weight = load(weight_ref, weight_v)
    load_bias = load(bias_ref, bias_v)
    load_cot = load(cot_ref, cot_v)

    near = [(1, 0), (3, 0), (0, 1), (2, 0), (1, 1), (3, 1), (2, 1)]
    barrier = pltpu.get_barrier_semaphore()
    partners = [sib]
    partners += [device(da=da, dz=dz) for da, dz in near]
    partners += [device(db=k) for k in (1, 2, 3)]
    partners += [device(drep=k) for k in (1, 2, 3)]
    for partner in partners:
        pl.semaphore_signal(barrier, inc=1, device_id=partner, device_id_type=MESH)
    load_feat.wait()
    pl.semaphore_wait(barrier, len(partners))

    def shard(i):
        return quart.at[pl.ds((i * 2 + c) * 2, 2)]

    def half(i, h):
        return quart.at[pl.ds((i * 2 + c) * 2 + h, 1)]

    def half_sem(i, h):
        return ag_sem.at[h * 32 + i]

    def to_axis(i, **where):
        send(shard(i), shard(i), ag_sem.at[i], device(**where), 1, 2)

    def along_b(da, dz):
        i = spot(da, 0, dz)
        to_axis(i, db=1)
        to_axis(i, db=3)
        if (da, dz) in DIRECT:
            to_axis(i, db=2)

    along_b(0, 0)
    for da, dz in ((0, 1), (1, 0), (3, 0), (2, 0), (1, 1), (3, 1)):
        to_axis(own, da=da, dz=dz)

    arrivals = [(k, j) for j in range(2) for k in (1, 3, 2)]
    order = ([(0, 0), (0, 1)] + arrivals)[::-1]
    rows = [((rep + 4 - k) % 4) * 2 + j for k, j in order]
    load_cols.wait()
    column = [lax.rem(cols_s[t % 2, rows[t // 2]], 128) for t in range(16)]
    lane = lax.broadcasted_iota(jnp.int32, (1, 128), 1)
    first = jnp.full((1, 128), 16, jnp.int32)
    for t in reversed(range(16)):
        first = jnp.where(lane == column[t], t, first)
    spots = jnp.zeros((1, 128), jnp.int32)
    for row in range(8):
        for k in range(2):
            spots = jnp.where(lane == row * 2 + k, lax.rem(cols_s[k, row], 128), spots)
    first_v[0, 0] = first
    first_v[0, 1] = spots
    first_copy = pltpu.make_async_remote_copy(
        src_ref=first_v.at[0], dst_ref=first_v.at[1], send_sem=send_sem.at[3], recv_sem=tab_sem,
        device_id=sib, device_id_type=MESH,
    )
    first_copy.start()

    def near_shard(da, dz):
        i = spot(da, 0, dz)
        arrive(shard(i), ag_sem.at[i])
        if (da, dz) == (0, 1):
            to_axis(i, da=2)
        along_b(da, dz)

    def beside(da, dz):
        for db, h, onward in ((3, 0, 1), (1, 1, 3)):
            i = spot(da, db, dz)
            arrive(shard(i), ag_sem.at[i])
            if (da, dz) not in DIRECT:
                send(half(i, h), half(i, h), half_sem(i, h), device(db=onward), 1, 1)

    def opposite(da, dz):
        i = spot(da, 2, dz)
        if (da, dz) in DIRECT:
            arrive(shard(i), ag_sem.at[i])
        else:
            arrive(half(i, 0), half_sem(i, 0))
            arrive(half(i, 1), half_sem(i, 1))

    load_vals.wait()
    send(vals_v, vals_sib, vals_sem, sib, 0, 16)
    todo = list(range(16))

    def transpose(n):
        for _ in range(n):
            t = todo.pop(0)
            vals_t[t] = vals_v[rows[t // 2] * 2 + t % 2].T

    transpose(4)
    near_shard(0, 1)
    near_shard(1, 0)
    near_shard(3, 0)
    beside(0, 0)
    near_shard(2, 0)
    near_shard(1, 1)
    near_shard(3, 1)
    beside(1, 0)
    beside(3, 0)
    beside(0, 1)
    near_shard(2, 1)
    transpose(2)
    beside(2, 0)
    transpose(2)
    beside(1, 1)
    transpose(2)
    beside(3, 1)
    transpose(2)
    opposite(0, 0)
    transpose(2)
    opposite(1, 0)
    transpose(2)
    opposite(3, 0)
    for t in range(16):
        following = jnp.int32(16)
        for u in reversed(range(t + 1, 16)):
            if u // 2 != t // 2:
                following = jnp.where(column[u] == column[t], u, following)
        next_s[t] = following
    acc[16] = jnp.zeros((BS, BS), F32)
    acc_b[16] = jnp.zeros((BS, BS), BF16)
    acc_sib[16] = jnp.zeros((BS, BS), BF16)
    quart[128] = jnp.zeros((BS, BS), BF16)
    arrive(first_v.at[1], tab_sem)
    table_copy = pltpu.make_async_copy(first_v, first_s, load_sem.at[6])
    table_copy.start()
    opposite(0, 1)
    opposite(2, 0)
    beside(2, 1)
    opposite(1, 1)
    opposite(3, 1)
    opposite(2, 1)
    arrive(vals_sib, vals_sem)
    table_copy.wait()

    def row_sum(vals, side, row):
        held = []
        for k in range(2):
            spot_at = first_s[side, 1, 0, row * 2 + k]
            held.append(quart[jnp.where((spot_at // 2) % 2 == c, spot_at, 128)])
        wide = jnp.concatenate([vals[row * 2], vals[row * 2 + 1]], axis=1)
        return jnp.dot(wide, jnp.concatenate(held, axis=0), preferred_element_type=F32)

    def targets(j):
        return [(k, ((rep + k) % 4) * 2 + j) for k in ORDER]

    for j in range(2):
        for k, row in targets(j):
            cross[k, j] = row_sum(vals_sib, 1, row)
        for k in ORDER:
            send(cross.at[k, j], cross_in.at[k, j], cross_sem.at[k, j], sib, 0, 2)
    own_sum = []
    for j in range(2):
        totals = [row_sum(vals_v, 0, row) for _, row in targets(j)]
        for k in ORDER:
            arrive(cross_in.at[k, j], cross_sem.at[k, j])
        for k, total in zip(ORDER, totals):
            total = total + cross_in[k, j]
            if k == 0:
                own_sum.append(total)
            else:
                part[k, j] = total.astype(BF16).reshape(2, 64, BS)
        for q in range(2):
            for k in (2, 1, 3):
                send(part.at[k, j, q], part_in.at[k, j, q], rep_sem.at[k - 1, j * 2 + q], device(drep=k), 0, 0.5)

    def reduce_rep(j, q):
        for k in (1, 3, 2):
            arrive(part_in.at[k, j, q], rep_sem.at[k - 1, j * 2 + q])
        total = own_sum[j][q * 64 : q * 64 + 64] + (
            part_in[1, j, q].astype(F32) + part_in[3, j, q].astype(F32) + part_in[2, j, q].astype(F32)
        )
        agg[rep * 2 + j, q] = total.astype(BF16)
        for k in (2, 1, 3):
            piece = agg.at[rep * 2 + j, q]
            send(piece, piece, repag_sem.at[k - 1, j * 2 + q], device(drep=k), 0, 0.5)

    def layer(pos):
        row = rows[pos]
        mine = agg[row].reshape(BS, BS)
        hidden = jnp.dot(mine, weight_v[...], preferred_element_type=F32) + bias_v[...]
        gate = jax.nn.sigmoid(hidden)
        out_v[row] = (hidden * gate).astype(BF16)
        pltpu.make_async_copy(out_v.at[row], out_ref.at[row], load_sem.at[7]).start()
        grad_hidden = (cot_v[row].astype(F32) * gate * (1.0 + hidden * (1.0 - gate))).astype(BF16)
        grad_rows = lax.dot_general(
            grad_hidden, weight_v[...], (((1,), (1,)), ((), ())), preferred_element_type=F32
        ).astype(BF16)
        for t in (pos * 2 + 1, pos * 2):
            term = jnp.dot(vals_t[t], grad_rows, preferred_element_type=F32) + acc[next_s[t]]
            acc[t] = term
            acc_b[t] = term.astype(BF16)
        send(acc_b.at[pl.ds(pos * 2, 2)], acc_sib.at[pl.ds(pos * 2, 2)], accsib_sem, sib, 2, 2)
        return lax.dot_general(mine, grad_hidden, (((0,), (0,)), ((), ())), preferred_element_type=F32) if pos > 5 else None

    def w_stage_near():
        arrive(wsib, w_sem.at[0])
        wa[pa * 2 + z] = wpart[c] + wsib[...]
        for n, (da, dz) in enumerate(near):
            send(wa.at[pa * 2 + z], wa.at[pa * 2 + z], w_sem.at[1 + n], device(da=da, dz=dz))

    def w_stage_b():
        for n, (da, dz) in enumerate(near):
            arrive(wa.at[((pa + 4 - da) % 4) * 2 + (z + dz) % 2], w_sem.at[1 + n])
        wb[pb] = ((wa[0] + wa[1]) + (wa[2] + wa[3])) + ((wa[4] + wa[5]) + (wa[6] + wa[7]))
        for k in (1, 2, 3):
            send(wb.at[pb], wb.at[pb], w_sem.at[7 + k], device(db=k))

    def w_stage_rep():
        for k in (1, 2, 3):
            arrive(wb.at[(pb + 4 - k) % 4], w_sem.at[7 + k])
        wr[rep] = (wb[0] + wb[1]) + (wb[2] + wb[3])
        for k in (1, 2, 3):
            send(wr.at[rep], wr.at[rep], w_sem.at[10 + k], device(drep=k))

    def w_stage_sib():
        for k in (1, 2, 3):
            arrive(wr.at[(rep + 4 - k) % 4], w_sem.at[10 + k])
        wfull[c] = (wr[0] + wr[1]) + (wr[2] + wr[3])
        send(wfull.at[c], wfull.at[c], w_sem.at[14], sib)

    load_weight.wait()
    load_bias.wait()
    load_cot.wait()
    reduce_rep(0, 0)
    reduce_rep(0, 1)
    product = layer(7)
    reduce_rep(1, 0)
    reduce_rep(1, 1)
    product = product + layer(6)
    wpart[0] = product[:64]
    wpart[1] = product[64:]
    send(wpart.at[1 - c], wsib, w_sem.at[0], sib)
    for n, (k, j) in enumerate(arrivals):
        for q in range(2):
            arrive(agg.at[rows[5 - n], q], repag_sem.at[k - 1, j * 2 + q])
        layer(5 - n)
        if n == 1:
            w_stage_near()
    arrive(acc_sib.at[pl.ds(0, 16)], accsib_sem)

    def place(ob, oa, zz):
        return ((ob * 4 + oa) * 2 + zz) * 2

    def build(ob, oa):
        for zz in range(2):
            i = flat((pa + oa) % 4, (pb + ob) % 4, zz)
            for blk in range(2):
                j = (i * 2 + c) * 2 + blk
                dense[place(ob, oa, zz) + blk] = acc_b[first_s[0, 0, 0, j]] + acc_sib[first_s[1, 0, 0, j]]

    def to_b(oa, ob, zz):
        side = 0 if ob == 1 else 1
        send(
            dense.at[pl.ds(place(ob, oa, zz), 2)], final_in.at[side, oa, zz], final_sem.at[side, oa], device(db=ob), 2, 2
        )

    for oa in ORDER:
        build(2, oa)
        send(dense.at[pl.ds(place(2, oa, 0), 2)], relay_in.at[0, oa], relay_sem.at[0, oa], device(db=1), 2, 2)
        send(dense.at[pl.ds(place(2, oa, 1), 2)], relay_in.at[1, oa], relay_sem.at[1, oa], device(db=3), 2, 2)
    for n, oa in enumerate(ORDER):
        build(1, oa)
        build(3, oa)
        if n == 0:
            to_b(oa, 1, 1)
            to_b(oa, 3, 0)
    w_stage_b()
    other = 1 - z

    def to_b_last(ob, zz):
        side = (ob - 1) // 2
        send(
            dense.at[pl.ds(place(ob, 0, zz), 2)], final_in.at[side, 0, zz], last_sem.at[side, zz], device(db=ob), 2, 2
        )

    def add_relay(side, ob, oa, zz):
        arrive(relay_in.at[side, oa], relay_sem.at[side, oa])
        at = pl.ds(place(ob, oa, zz), 2)
        dense[at] = (dense[at].astype(F32) + relay_in[side, oa].astype(F32)).astype(BF16)

    for n, oa in enumerate(ORDER[:3]):
        for side, ob, zz in ((0, 1, 0), (1, 3, 1)):
            add_relay(side, ob, oa, zz)
            to_b(oa, ob, zz)
        if n < 2:
            to_b(ORDER[n + 1], 1, 1)
            to_b(ORDER[n + 1], 3, 0)
    to_b_last(3 - 2 * other, other)
    add_relay(other, 1 + 2 * other, 0, other)
    to_b_last(1 + 2 * other, other)
    to_b_last(3 - 2 * z, z)
    add_relay(z, 1 + 2 * z, 0, z)
    to_b_last(1 + 2 * z, z)
    w_stage_rep()
    for oa in ORDER:
        build(0, oa)

    def sum_b(oa, zz):
        return dense[pl.ds(place(0, oa, zz), 2)].astype(F32) + (
            final_in[0, oa, zz].astype(F32) + final_in[1, oa, zz].astype(F32)
        )

    def to_near(oa, dz):
        slot = oa * 2 + dz
        send(summed.at[oa, (z + dz) % 2], near_in.at[slot], near_sem.at[slot], device(da=oa, dz=dz), 2, 2)

    for oa in ORDER[:3]:
        for side in range(2):
            arrive(final_in.at[side, oa], final_sem.at[side, oa])
        for zz in range(2):
            summed[oa, zz] = sum_b(oa, zz).astype(BF16)
        to_near(oa, 1)
        to_near(oa, 0)
    for side in range(2):
        arrive(final_in.at[side, 0, other], last_sem.at[side, other])
    summed[0, other] = sum_b(0, other).astype(BF16)
    to_near(0, 1)
    w_stage_sib()
    for side in range(2):
        arrive(final_in.at[side, 0, z], last_sem.at[side, z])
    total = sum_b(0, z)
    for oa in ORDER:
        for dz in (0, 1):
            if oa or dz:
                slot = oa * 2 + dz
                arrive(near_in.at[slot], near_sem.at[slot])
                total = total + near_in[slot].astype(F32)
    fg_v[...] = total
    fgrad_copy = pltpu.make_async_copy(fg_v, fgrad_ref, load_sem.at[8])
    fgrad_copy.start()
    arrive(wfull.at[1 - c], w_sem.at[14])
    wgrad_copy = pltpu.make_async_copy(wfull, wgrad_ref, load_sem.at[9])
    wgrad_copy.start()
    for group, blocks in enumerate(sent):
        assert blocks <= 128 and blocks == int(blocks)
        ref = quart.at[pl.ds(0, int(blocks))]
        pltpu.make_async_remote_copy(
            src_ref=ref, dst_ref=ref, send_sem=send_sem.at[group], recv_sem=tab_sem, device_id=sib, device_id_type=MESH
        ).wait_send()
    first_copy.wait_send()
    pltpu.make_async_copy(out_v, out_ref, load_sem.at[7]).wait()
    fgrad_copy.wait()
    wgrad_copy.wait()


def emit(out_in, fgrad_in, wgrad_in, out_ref, fgrad_ref, wgrad_ref, sem):
    copies = [
        pltpu.make_async_copy(src, dst, sem.at[n])
        for n, (src, dst) in enumerate(((out_in, out_ref), (fgrad_in, fgrad_ref), (wgrad_in, wgrad_ref)))
    ]
    for copy in copies:
        copy.start()
    for copy in copies:
        copy.wait()


def body(cols, vals, features, weight, bias, cotangent):
    anywhere = pl.BlockSpec(memory_space=pl.ANY)
    vmem = pltpu.VMEM
    dma = pltpu.SemaphoreType.DMA
    block = (BS, BS)
    scratch = [
        pltpu.SMEM((2, 8), jnp.int32),
        pltpu.SMEM((2, 2, 1, 128), jnp.int32),
        pltpu.SMEM((16,), jnp.int32),
        vmem((16, *block), BF16),
        vmem((16, *block), BF16),
        vmem((16, *block), BF16),
        vmem(block, BF16),
        vmem((1, BS), F32),
        vmem((8, *block), BF16),
        vmem((2, 2, 1, 128), jnp.int32),
        vmem((129, *block), BF16),
        vmem((4, 2, *block), F32),
        vmem((4, 2, *block), F32),
        vmem((4, 2, 2, 64, BS), BF16),
        vmem((4, 2, 2, 64, BS), BF16),
        vmem((8, 2, 64, BS), BF16),
        vmem((8, *block), BF16),
        vmem((2, 64, BS), F32),
        vmem((64, BS), F32),
        vmem((8, 64, BS), F32),
        vmem((4, 64, BS), F32),
        vmem((4, 64, BS), F32),
        vmem((2, 64, BS), F32),
        vmem((17, *block), F32),
        vmem((17, *block), BF16),
        vmem((17, *block), BF16),
        vmem((64, *block), BF16),
        vmem((2, 4, 2, *block), BF16),
        vmem((2, 4, 2, 2, *block), BF16),
        vmem((4, 2, 2, *block), BF16),
        vmem((8, 2, *block), BF16),
        vmem((2, *block), F32),
        dma((10,)),
        dma((4,)),
        dma((64,)),
        dma((4, 2)),
        dma,
        dma,
        dma((3, 4)),
        dma((3, 4)),
        dma((15,)),
        dma,
        dma((2, 4)),
        dma((2, 4)),
        dma((2, 2)),
        dma((8,)),
    ]
    results = (
        jax.ShapeDtypeStruct((8, *block), BF16),
        jax.ShapeDtypeStruct((2, *block), F32),
        jax.ShapeDtypeStruct((2, 64, BS), F32),
    )
    operands = (
        cols.T,
        vals.reshape(16, *block),
        features.reshape(2, *block),
        weight,
        bias.reshape(1, BS),
        cotangent.reshape(8, *block),
    )
    outs = pl.pallas_call(
        kernel,
        out_shape=results,
        in_specs=[anywhere] * 6,
        out_specs=(anywhere,) * 3,
        scratch_shapes=scratch,
        compiler_params=pltpu.CompilerParams(
            collective_id=0, has_side_effects=True, vmem_limit_bytes=32 << 20
        ),
    )(*[pltpu.with_memory_space_constraint(operand, pltpu.HBM) for operand in operands])
    output, feature_grad, weight_grad = pl.pallas_call(
        emit,
        out_shape=results,
        in_specs=[anywhere] * 3,
        out_specs=(anywhere,) * 3,
        scratch_shapes=[dma((3,))],
    )(*[pltpu.with_memory_space_constraint(out, pltpu.VMEM) for out in outs])
    return output.reshape(1024, BS), feature_grad.reshape(256, BS), weight_grad.reshape(BS, BS)


def solution(mesh):
    placed = (
        P("dom", "rep"),
        P("dom", "rep", None, None),
        P(("rep", "dom"), None),
        P(),
        P(),
        P("dom", None),
    )
    return jax.shard_map(
        body,
        mesh=mesh,
        in_specs=placed,
        out_specs=(P("dom", None), P(("rep", "dom"), None), P()),
        check_vma=False,
    )
```
